32 devices in a mesh: blk: 8 (over z, y), plane: 4 (over x, core).
Axes of the slice: x: 2, y: 2, z: 4, core: 2. Of those that a mesh axis runs over, the one named last changes fastest.
Arguments:
- tiles: bfloat16 [128, 24, 128, 128], P(('blk', 'plane')), may hold values from -0.25 to 0.25
- tile_cols: int32 [128, 24], P(('blk', 'plane')), may hold values from 0 to 511
- tile_count: int32 [128], P(('blk', 'plane')), may hold values from 18 to 24, as said below
- u_start: float32 [16384], P(('blk', 'plane')), may hold values from -0.046875 to 0.046875
- v_start: float32 [65536], P(('blk', 'plane')), may hold values from -0.0234375 to 0.0234375
- beta_start: float32 [1], replicated, may hold values from 0.5 to 1.5
- left_basis: float32 [16384, 128], P(('blk', 'plane')), may hold values from -0.046875 to 0.046875
- right_basis: float32 [65536, 128], P(('blk', 'plane')), may hold values from -0.0234375 to 0.0234375
Outputs:
- left_vectors: float32 [1, 16384], P(None, ('blk', 'plane'))
- right_vectors: float32 [1, 65536], P(None, ('blk', 'plane'))
- coefficients: float32 [2], replicated
The draws below stay inside these ranges and needn't reach their ends.
Inputs may be any that keep to these rules, and one draw needn't show every extreme that they name: `tile_count`: slots at and after a row block's count are padding; some row block uses all 24 slots.
All inputs are finite; a program needn't handle non-finite values.
Results may differ from the reference program's by a relative error of at most 0.00055.
The reference program's roundings to bfloat16 on the way count: a program that leaves them out, or rounds other values in their place, can miss the bound.
Values may be sent and summed in bfloat16 or wider, within the bound.
No kernel may reach another device: no remote copies, remote signals or barrier semaphores. Data moves between devices by JAX's collectives and lax.ppermute only.
A program may use at most 64 MiB of HBM per device.

```python
import jax
import jax.numpy as jnp
from jax import lax

N = 65536
NT = 512
SLOTS = 24
KB = 128
ITERS = 1
BLOCKS = 128
ROWS = 16384


def draw_tile_count(key, part):
    counts = jax.random.randint(key, (BLOCKS,), max(1, 3 * SLOTS // 4), SLOTS + 1).astype(jnp.int32)
    return counts.at[0].set(SLOTS)


def plant(drawn, own_key, smallest, top_value):
    dims = drawn.shape
    spot = [jax.random.randint(jax.random.fold_in(own_key, axis), (), 0, dims[axis]) for axis in range(len(dims))]
    drawn = drawn.at[tuple(spot)].set(smallest)
    longest = dims.index(max(dims))
    spot[longest] = (spot[longest] + 1) % dims[longest]
    return drawn.at[tuple(spot)].set(top_value)


def block_scale(stream_key, extent, cuts, low, largest):
    level, own = 1.0, jax.random.fold_in(stream_key, 6)
    for position, shards_of in cuts:
        draws = jnp.exp(jax.random.uniform(jax.random.fold_in(own, position), (shards_of,), jnp.float32, low / len(cuts), largest / len(cuts)))
        level = level * jnp.repeat(draws, extent[position] // shards_of).reshape([-1 if axis == position else 1 for axis in range(len(extent))])
    return level


def centred(rng, shape, spread, limit, shards=(), kind=jnp.bfloat16):
    drawn = spread * jax.random.normal(rng, shape, jnp.float32)
    if shards:
        drawn = drawn * block_scale(rng, shape, shards, -0.22, 0.18)
    return jnp.clip(drawn, -limit, limit).astype(kind)


def setup_inputs(seed: int = 0) -> dict:
    key_of = jax.random.split(jax.random.key(seed), 9)
    tiles = centred(key_of[0], (BLOCKS, SLOTS, 128, 128), (ROWS * SLOTS * 112 // N) ** -0.5, 0.25, ((0, 32),))
    tile_cols = plant(jax.random.randint(key_of[1], (BLOCKS, SLOTS), 0, NT), jax.random.fold_in(key_of[1], 1), 0, NT - 1).astype(jnp.int32)
    tile_count = draw_tile_count(jax.random.fold_in(key_of[8], 71), 0)
    u_start = centred(key_of[3], (ROWS,), ROWS ** -0.5, 0.046875, ((0, 32),), jnp.float32)
    v_start = centred(key_of[4], (N,), N ** -0.5, 0.0234375, ((0, 32),), jnp.float32)
    beta_start = jnp.clip(jax.random.uniform(key_of[5], (1,), jnp.float32, 0.5, 1.5), 0.5, 1.5)
    left_basis = centred(key_of[6], (ROWS, KB), ROWS ** -0.5, 0.046875, ((0, 32),), jnp.float32)
    right_basis = centred(key_of[7], (N, KB), N ** -0.5, 0.0234375, ((0, 32),), jnp.float32)
    return dict(tiles=tiles, tile_cols=tile_cols, tile_count=tile_count, u_start=u_start, v_start=v_start, beta_start=beta_start, left_basis=left_basis, right_basis=right_basis)


def project_twice(vec, basis):
    high = lax.Precision.HIGHEST
    first = jnp.dot(vec, basis, precision=high)
    vec = vec - jnp.dot(basis, first, precision=high)
    second = jnp.dot(vec, basis, precision=high)
    vec = vec - jnp.dot(basis, second, precision=high)
    norm = jnp.sqrt(jnp.sum(vec * vec) + 1e-06)
    return (vec / norm, norm)

def reference(tiles, tile_cols, tile_count, u_start, v_start, beta_start, left_basis, right_basis):
    high = lax.Precision.HIGHEST
    live = (jnp.arange(SLOTS, dtype=jnp.int32)[None, :] < tile_count[:, None]).astype(jnp.float32)

    def forward(rounded):
        table = rounded.reshape(-1, 128)

        def single(items):
            block, cols, weight = items
            picked = table[cols].astype(jnp.float32)
            values = jnp.einsum('sij,sj->si', block.astype(jnp.float32), picked, precision=high)
            return lax.optimization_barrier(jnp.sum(values * weight[:, None], axis=0))
        return lax.map(single, (tiles, tile_cols, live)).reshape(-1)

    def backward(rounded):
        table = rounded.reshape(-1, 128)

        def single(items):
            block, row, weight = items
            values = jnp.einsum('sij,i->sj', block.astype(jnp.float32), row.astype(jnp.float32), precision=high)
            return values * weight[:, None]
        contrib = lax.map(single, (tiles, table, live)).reshape(-1, 128)
        summed = jax.ops.segment_sum(contrib, tile_cols.reshape(-1), num_segments=N // 128)
        return summed.reshape(-1)
    vec_right = v_start
    vec_left = u_start
    beta = beta_start[0]
    lefts, rights, coefs = ([], [], [])
    for step in range(ITERS):
        forward_out = forward(vec_right.astype(jnp.bfloat16))
        vec_left, alpha = project_twice(forward_out - beta * vec_left, left_basis)
        back_out = backward(vec_left.astype(jnp.bfloat16))
        vec_right, beta = project_twice(back_out - alpha * vec_right, right_basis)
        lefts.append(vec_left * jnp.sqrt(jnp.float32(ROWS)))
        rights.append(vec_right * jnp.sqrt(jnp.float32(N)))
        coefs.append(alpha)
        coefs.append(beta)
    return (jnp.stack(lefts), jnp.stack(rights), jnp.stack(coefs))
```

```python
import math

import jax
import jax.numpy as jnp
from jax import lax
from jax.sharding import PartitionSpec as P

AXES = ("blk", "plane")


def exchange(parts):
    return lax.all_to_all(parts, AXES, 0, 0, tiled=True)


def spread(rows, devices):
    return jnp.broadcast_to(rows[None], (devices,) + rows.shape)


def finish(vec, basis, gram, first, whole_sq):
    high = lax.Precision.HIGHEST
    coef = 2.0 * first - jnp.dot(gram, first, precision=high)
    vec = vec - jnp.dot(basis, coef, precision=high)
    total = (
        whole_sq - 2.0 * jnp.sum(coef * first) + jnp.sum(coef * jnp.dot(gram, coef, precision=high))
    )
    norm = jnp.sqrt(total + 1e-06)
    return (vec / norm, norm)


def inner(vec, basis):
    first = jnp.dot(vec, basis, precision=lax.Precision.HIGHEST)
    square = jnp.broadcast_to(jnp.sum(vec * vec), first.shape)
    return jnp.stack([first, square])


def on_device(tiles, tile_cols, tile_count, u_start, v_start, beta_start, left_basis, right_basis):
    high = lax.Precision.HIGHEST
    devices = lax.axis_size(AXES)
    blocks, slots = tile_cols.shape
    width = tiles.shape[-1]
    kept = left_basis.shape[1]
    own_tiles = v_start.shape[0] // width
    n_tiles = own_tiles * devices
    live = (lax.iota(jnp.int32, slots)[None, :] < tile_count[:, None]).astype(jnp.float32)
    onehot = (tile_cols.reshape(-1)[:, None] == lax.iota(jnp.int32, n_tiles)[None, :]).astype(
        jnp.float32
    )
    left_scale = math.sqrt(u_start.shape[0] * devices)
    right_scale = math.sqrt(v_start.shape[0] * devices)
    beta = beta_start[0]

    grams = jnp.concatenate(
        [
            jnp.dot(left_basis.T, left_basis, precision=high),
            jnp.dot(right_basis.T, right_basis, precision=high),
        ]
    )
    share = 2 * kept // devices
    rounded = lax.reduce_precision(v_start, 8, 7).reshape(own_tiles, width)
    got = exchange(
        jnp.concatenate([grams.reshape(devices, share, kept), spread(rounded, devices)], axis=1)
    )
    gram_rows = jnp.sum(got[:, :share], axis=0)
    table = got[:, share:].reshape(n_tiles, width).astype(jnp.bfloat16)
    picked = jnp.take(table, tile_cols, axis=0)
    values = jnp.einsum("rsij,rsj->rsi", tiles, picked, preferred_element_type=jnp.float32)
    forward_out = jnp.sum(values * live[:, :, None], axis=1).reshape(-1)
    vec_left = forward_out - beta * u_start

    got = exchange(spread(jnp.concatenate([gram_rows, inner(vec_left, left_basis)]), devices))
    whole_grams = got[:, :share].reshape(2 * kept, kept)
    sums = jnp.sum(got[:, share:], axis=0)
    vec_left, alpha = finish(vec_left, left_basis, whole_grams[:kept], sums[0], sums[1, 0])

    left_rows = vec_left.astype(jnp.bfloat16).reshape(blocks, width)
    contrib = jnp.einsum("rsij,ri->rsj", tiles, left_rows, preferred_element_type=jnp.float32)
    contrib = (contrib * live[:, :, None]).reshape(-1, width)
    partial_value = lax.dot_general(onehot, contrib, (((0,), (0,)), ((), ())), precision=high)
    got = exchange(partial_value.reshape(devices, own_tiles, width))
    back_out = jnp.sum(got, axis=0).reshape(-1)
    vec_right = back_out - alpha * v_start

    got = exchange(spread(inner(vec_right, right_basis), devices))
    sums = jnp.sum(got, axis=0)
    vec_right, beta = finish(vec_right, right_basis, whole_grams[kept:], sums[0], sums[1, 0])
    return (
        (vec_left * left_scale)[None],
        (vec_right * right_scale)[None],
        jnp.stack([alpha, beta]),
    )


def solution(mesh):
    placed = (
        P(AXES, None, None, None),
        P(AXES, None),
        P(AXES),
        P(AXES),
        P(AXES),
        P(),
        P(AXES, None),
        P(AXES, None),
    )
    return jax.shard_map(
        on_device,
        mesh=mesh,
        in_specs=placed,
        out_specs=(P(None, AXES), P(None, AXES), P()),
        check_vma=False,
    )
```

```python
import math
from functools import partial

import jax
import jax.numpy as jnp
from jax import lax
from jax.experimental import pallas as pl
from jax.experimental.pallas import tpu as pltpu
from jax.sharding import PartitionSpec as P

AXES = ("blk", "plane")
F32 = jnp.float32


def exchange(parts):
    return lax.all_to_all(parts, AXES, 0, 0, tiled=True)


def column(row):
    size = row.shape[1]
    return jnp.broadcast_to(row, (size, size)).T


def left_times(row, mat):
    return jnp.sum(mat * column(row), axis=0, keepdims=True)


def right_times(mat, row):
    return jnp.sum((mat * row).T, axis=0, keepdims=True)


def total_of(row):
    return jnp.sum(row, axis=1, keepdims=True)


def forward_kernel(cols, counts, beta, got, tiles, basis, u_prev, payload, p_out, first, square):
    b = pl.program_id(0)
    share = payload.shape[1] - 2
    own = got.shape[1] - share
    slots, width = tiles.shape[1], tiles.shape[2]

    @pl.when(b == 0)
    def _():
        first[...] = jnp.zeros_like(first)
        square[...] = jnp.zeros_like(square)

    acc = jnp.zeros((width, width), F32)
    for s in range(slots):
        col = cols[b, s]
        row = got[lax.div(col, own), pl.ds(share + lax.rem(col, own), 1), :]
        row = jnp.where(s < counts[b], row, 0.0)
        acc = acc + tiles[0, s].astype(F32) * row
    p = jnp.sum(acc.T, axis=0, keepdims=True) - beta[0] * u_prev[pl.ds(b, 1), :]
    p_out[pl.ds(b, 1), :] = p
    first[...] += left_times(p, basis[0])
    square[...] += p * p

    @pl.when(b == pl.num_programs(0) - 1)
    def _():
        gram = jnp.sum(got[:, :share, :], axis=0)
        payload[:, :share, :] = jnp.broadcast_to(gram[None], (payload.shape[0],) + gram.shape)
        tail = (payload.shape[0], 1, width)
        payload[:, share : share + 1, :] = jnp.broadcast_to(first[...][None], tail)
        payload[:, share + 1 :, :] = jnp.broadcast_to(square[...][None], tail)


def solve(gram, sums):
    first = sums[0:1]
    coef = 2.0 * first - left_times(first, gram)
    total = (
        total_of(sums[1:2])
        - 2.0 * total_of(coef * first)
        + total_of(coef * left_times(coef, gram))
    )
    return coef, jnp.sqrt(total + 1e-06)


def fill_gram(gram, got, start, share):
    for d in range(gram.shape[0] // share):
        gram[d * share : (d + 1) * share, :] = got[start + d, :share, :]


def backward_kernel(
    cols, counts, got, p_in, tiles, basis, partial_out, u_out, alpha, gram, coef, *, scale
):
    b = pl.program_id(0)
    share = got.shape[1] - 2
    slots = tiles.shape[1]

    @pl.when(b == 0)
    def _():
        partial_out[...] = jnp.zeros_like(partial_out)
        fill_gram(gram, got, 0, share)
        found, norm = solve(gram[...], jnp.sum(got[:, share:, :], axis=0))
        coef[...] = found
        alpha[...] = jnp.broadcast_to(norm, alpha.shape)

    u = (p_in[pl.ds(b, 1), :] - right_times(basis[0], coef[...])) / alpha[...]
    u_out[pl.ds(b, 1), :] = u * scale
    spread = column(u.astype(jnp.bfloat16).astype(F32))
    for s in range(slots):
        part = jnp.sum(tiles[0, s].astype(F32) * spread, axis=0, keepdims=True)
        part = jnp.where(s < counts[b], part, 0.0)
        at = pl.ds(cols[b, s], 1)
        partial_out[at, :] = partial_out[at, :] + part


def inner_kernel(got, v_prev, alpha, basis, payload, r_out):
    r = jnp.sum(got[...], axis=0) - alpha[...] * v_prev[...]
    r_out[...] = r
    first = left_times(r[0:1], basis[0])
    for b in range(1, basis.shape[0]):
        first = first + left_times(r[b : b + 1], basis[b])
    tail = (payload.shape[0], 1, payload.shape[2])
    payload[:, 0:1, :] = jnp.broadcast_to(first[None], tail)
    square = jnp.sum(r * r, axis=0, keepdims=True)
    payload[:, 1:2, :] = jnp.broadcast_to(square[None], tail)


def final_kernel(got, grams, r_in, alpha, basis, v_out, coefs, gram, *, scale):
    share = grams.shape[1] - 2
    fill_gram(gram, grams, grams.shape[0] // 2, share)
    coef, norm = solve(gram[...], jnp.sum(got[...], axis=0))
    for b in range(basis.shape[0]):
        v = (r_in[b : b + 1, :] - right_times(basis[b], coef)) / norm
        v_out[b : b + 1, :] = v * scale
    coefs[0] = jnp.max(alpha[...])
    coefs[1] = jnp.max(norm)


def on_device(tiles, tile_cols, tile_count, u_start, v_start, beta_start, left_basis, right_basis):
    high = lax.Precision.HIGHEST
    devices = lax.axis_size(AXES)
    blocks, slots = tile_cols.shape
    width = tiles.shape[-1]
    kept = left_basis.shape[1]
    own = v_start.shape[0] // width
    n_tiles = own * devices
    left_scale = math.sqrt(u_start.shape[0] * devices)
    right_scale = math.sqrt(v_start.shape[0] * devices)
    share = 2 * kept // devices
    shape = jax.ShapeDtypeStruct
    smem = pl.BlockSpec(memory_space=pltpu.SMEM)
    vmem = pl.BlockSpec(memory_space=pltpu.VMEM)
    tile_spec = pl.BlockSpec((1, slots, width, width), lambda b: (b, 0, 0, 0))
    basis_spec = pl.BlockSpec((1, width, kept), lambda b: (b, 0, 0))
    left = left_basis.reshape(blocks, width, kept)
    right = right_basis.reshape(own, width, kept)
    row = pltpu.VMEM((1, kept), F32)

    grams = jnp.concatenate(
        [
            jnp.dot(left_basis.T, left_basis, precision=high),
            jnp.dot(right_basis.T, right_basis, precision=high),
        ]
    )
    v_rows = v_start.reshape(own, width)
    rounded = lax.reduce_precision(v_rows, 8, 7)
    got = exchange(
        jnp.concatenate(
            [
                grams.reshape(devices, share, kept),
                jnp.broadcast_to(rounded[None], (devices, own, width)),
            ],
            axis=1,
        )
    )
    payload, p = pl.pallas_call(
        forward_kernel,
        grid=(blocks,),
        in_specs=[smem, smem, smem, vmem, tile_spec, basis_spec, vmem],
        out_specs=[vmem, vmem],
        out_shape=[shape((devices, share + 2, width), F32), shape((blocks, width), F32)],
        scratch_shapes=[row, row],
        name="forward",
    )(tile_cols, tile_count, beta_start, got, tiles, left, u_start.reshape(blocks, width))
    sums = exchange(payload)
    partial_sums, u, alpha = pl.pallas_call(
        partial(backward_kernel, scale=left_scale),
        grid=(blocks,),
        in_specs=[smem, smem, vmem, vmem, tile_spec, basis_spec],
        out_specs=[vmem, vmem, vmem],
        out_shape=[
            shape((n_tiles, width), F32),
            shape((blocks, width), F32),
            shape((1, width), F32),
        ],
        scratch_shapes=[pltpu.VMEM((kept, kept), F32), row],
        name="backward",
    )(tile_cols, tile_count, sums, p, tiles, left)
    got = exchange(partial_sums.reshape(devices, own, width))
    payload, r = pl.pallas_call(
        inner_kernel,
        in_specs=[vmem] * 4,
        out_specs=[vmem, vmem],
        out_shape=[shape((devices, 2, width), F32), shape((own, width), F32)],
        name="inner",
    )(got, v_rows, alpha, right)
    v, coefs = pl.pallas_call(
        partial(final_kernel, scale=right_scale),
        in_specs=[vmem] * 5,
        out_specs=[vmem, smem],
        out_shape=[shape((own, width), F32), shape((2,), F32)],
        scratch_shapes=[pltpu.VMEM((kept, kept), F32)],
        name="final",
    )(exchange(payload), sums, r, alpha, right)
    return u.reshape(1, -1), v.reshape(1, -1), coefs


def solution(mesh):
    placed = (
        P(AXES, None, None, None),
        P(AXES, None),
        P(AXES),
        P(AXES),
        P(AXES),
        P(),
        P(AXES, None),
        P(AXES, None),
    )
    return jax.shard_map(
        on_device,
        mesh=mesh,
        in_specs=placed,
        out_specs=(P(None, AXES), P(None, AXES), P()),
        check_vma=False,
    )
```

```python
import math
from functools import partial

import jax
import jax.numpy as jnp
from jax import lax
from jax.experimental import pallas as pl
from jax.experimental.pallas import tpu as pltpu
from jax.sharding import PartitionSpec as P

AXES = ("blk", "plane")
F32 = jnp.float32


def exchange(parts):
    return lax.all_to_all(parts, AXES, 0, 0, tiled=True)


def column(row):
    size = row.shape[1]
    return jnp.broadcast_to(row, (size, size)).T


def left_times(row, mat):
    return jnp.sum(mat * column(row), axis=0, keepdims=True)


def right_times(mat, row):
    return jnp.sum((mat * row).T, axis=0, keepdims=True)


def total_of(row):
    return jnp.sum(row, axis=1, keepdims=True)


def forward_kernel(
    cols, counts, beta, got, tiles, basis, u_prev, payload, p_out, kept_rows, first, square
):
    b = pl.program_id(0)
    share = payload.shape[1] - 2
    own = got.shape[1] - 2 * share
    slots, width = tiles.shape[1], tiles.shape[2]

    @pl.when(b == 0)
    def _():
        first[...] = jnp.zeros_like(first)
        square[...] = jnp.zeros_like(square)

    acc = jnp.zeros((width, width), F32)
    for s in range(slots):
        col = cols[b, s]
        row = got[lax.div(col, own), pl.ds(2 * share + lax.rem(col, own), 1), :]
        row = jnp.where(s < counts[b], row, 0.0)
        acc = acc + tiles[0, s].astype(F32) * row
    p = jnp.sum(acc.T, axis=0, keepdims=True) - beta[0] * u_prev[pl.ds(b, 1), :]
    p_out[pl.ds(b, 1), :] = p
    first[...] += left_times(p, basis[0])
    square[...] += p * p

    @pl.when(b == pl.num_programs(0) - 1)
    def _():
        gram = jnp.sum(got[:, :share, :], axis=0)
        payload[:, :share, :] = jnp.broadcast_to(gram[None], (payload.shape[0],) + gram.shape)
        kept_rows[...] = jnp.sum(got[:, share : 2 * share, :], axis=0)
        tail = (payload.shape[0], 1, width)
        payload[:, share : share + 1, :] = jnp.broadcast_to(first[...][None], tail)
        payload[:, share + 1 :, :] = jnp.broadcast_to(square[...][None], tail)


def solve(gram, sums):
    first = sums[0:1]
    coef = 2.0 * first - left_times(first, gram)
    total = (
        total_of(sums[1:2])
        - 2.0 * total_of(coef * first)
        + total_of(coef * left_times(coef, gram))
    )
    return coef, jnp.sqrt(total + 1e-06)


def fill_gram(gram, got, share):
    for d in range(gram.shape[0] // share):
        gram[d * share : (d + 1) * share, :] = got[d, :share, :]


def backward_kernel(
    cols, counts, got, p_in, tiles, basis, partial_out, u_out, alpha, gram, coef, *, scale
):
    b = pl.program_id(0)
    share = got.shape[1] - 2
    slots = tiles.shape[1]

    @pl.when(b == 0)
    def _():
        partial_out[...] = jnp.zeros_like(partial_out)
        fill_gram(gram, got, share)
        found, norm = solve(gram[...], jnp.sum(got[:, share:, :], axis=0))
        coef[...] = found
        alpha[...] = jnp.broadcast_to(norm, alpha.shape)

    u = (p_in[pl.ds(b, 1), :] - right_times(basis[0], coef[...])) / alpha[...]
    u_out[pl.ds(b, 1), :] = u * scale
    spread = column(u.astype(jnp.bfloat16).astype(F32))
    for s in range(slots):
        part = jnp.sum(tiles[0, s].astype(F32) * spread, axis=0, keepdims=True)
        part = jnp.where(s < counts[b], part, 0.0)
        at = pl.ds(cols[b, s], 1)
        partial_out[at, :] = partial_out[at, :] + part


def inner_kernel(got, v_prev, alpha, basis, gram_rows, payload, r_out):
    share = gram_rows.shape[0]
    r = jnp.sum(got[...], axis=0) - alpha[...] * v_prev[...]
    r_out[...] = r
    first = left_times(r[0:1], basis[0])
    for b in range(1, basis.shape[0]):
        first = first + left_times(r[b : b + 1], basis[b])
    tail = (payload.shape[0], 1, payload.shape[2])
    payload[:, :share, :] = jnp.broadcast_to(
        gram_rows[...][None], (payload.shape[0],) + gram_rows.shape
    )
    payload[:, share : share + 1, :] = jnp.broadcast_to(first[None], tail)
    square = jnp.sum(r * r, axis=0, keepdims=True)
    payload[:, share + 1 :, :] = jnp.broadcast_to(square[None], tail)


def final_kernel(got, r_in, alpha, basis, v_out, coefs, gram, *, scale):
    share = got.shape[1] - 2
    fill_gram(gram, got, share)
    coef, norm = solve(gram[...], jnp.sum(got[:, share:, :], axis=0))
    for b in range(basis.shape[0]):
        v = (r_in[b : b + 1, :] - right_times(basis[b], coef)) / norm
        v_out[b : b + 1, :] = v * scale
    coefs[0] = jnp.max(alpha[...])
    coefs[1] = jnp.max(norm)


def on_device(tiles, tile_cols, tile_count, u_start, v_start, beta_start, left_basis, right_basis):
    high = lax.Precision.HIGHEST
    devices = lax.axis_size(AXES)
    blocks, slots = tile_cols.shape
    width = tiles.shape[-1]
    kept = left_basis.shape[1]
    own = v_start.shape[0] // width
    n_tiles = own * devices
    left_scale = math.sqrt(u_start.shape[0] * devices)
    right_scale = math.sqrt(v_start.shape[0] * devices)
    share = pl.cdiv(kept, devices)
    shape = jax.ShapeDtypeStruct
    smem = pl.BlockSpec(memory_space=pltpu.SMEM)
    vmem = pl.BlockSpec(memory_space=pltpu.VMEM)
    tile_spec = pl.BlockSpec((1, slots, width, width), lambda b: (b, 0, 0, 0))
    basis_spec = pl.BlockSpec((1, width, kept), lambda b: (b, 0, 0))
    left = left_basis.reshape(blocks, width, kept)
    right = right_basis.reshape(own, width, kept)
    row = pltpu.VMEM((1, kept), F32)

    def shares(basis):
        gram = jnp.dot(basis.T, basis, precision=high)
        gram = jnp.pad(gram, ((0, share * devices - kept), (0, 0)))
        return gram.reshape(devices, share, kept)

    v_rows = v_start.reshape(own, width)
    rounded = lax.reduce_precision(v_rows, 8, 7)
    got = exchange(
        jnp.concatenate(
            [
                shares(left_basis),
                shares(right_basis),
                jnp.broadcast_to(rounded[None], (devices, own, width)),
            ],
            axis=1,
        )
    )
    payload, p, kept_rows = pl.pallas_call(
        forward_kernel,
        grid=(blocks,),
        in_specs=[smem, smem, smem, vmem, tile_spec, basis_spec, vmem],
        out_specs=[vmem, vmem, vmem],
        out_shape=[
            shape((devices, share + 2, width), F32),
            shape((blocks, width), F32),
            shape((share, width), F32),
        ],
        scratch_shapes=[row, row],
        name="forward",
    )(tile_cols, tile_count, beta_start, got, tiles, left, u_start.reshape(blocks, width))
    sums = exchange(payload)
    partial_sums, u, alpha = pl.pallas_call(
        partial(backward_kernel, scale=left_scale),
        grid=(blocks,),
        in_specs=[smem, smem, vmem, vmem, tile_spec, basis_spec],
        out_specs=[vmem, vmem, vmem],
        out_shape=[
            shape((n_tiles, width), F32),
            shape((blocks, width), F32),
            shape((1, width), F32),
        ],
        scratch_shapes=[pltpu.VMEM((kept, kept), F32), row],
        name="backward",
    )(tile_cols, tile_count, sums, p, tiles, left)
    got = exchange(partial_sums.reshape(devices, own, width))
    payload, r = pl.pallas_call(
        inner_kernel,
        in_specs=[vmem] * 5,
        out_specs=[vmem, vmem],
        out_shape=[shape((devices, share + 2, width), F32), shape((own, width), F32)],
        name="inner",
    )(got, v_rows, alpha, right, kept_rows)
    v, coefs = pl.pallas_call(
        partial(final_kernel, scale=right_scale),
        in_specs=[vmem] * 4,
        out_specs=[vmem, smem],
        out_shape=[shape((own, width), F32), shape((2,), F32)],
        scratch_shapes=[pltpu.VMEM((kept, kept), F32)],
        name="final",
    )(exchange(payload), r, alpha, right)
    return u.reshape(1, -1), v.reshape(1, -1), coefs


def solution(mesh):
    placed = (
        P(AXES, None, None, None),
        P(AXES, None),
        P(AXES),
        P(AXES),
        P(AXES),
        P(),
        P(AXES, None),
        P(AXES, None),
    )
    return jax.shard_map(
        on_device,
        mesh=mesh,
        in_specs=placed,
        out_specs=(P(None, AXES), P(None, AXES), P()),
        check_vma=False,
    )
```
